256 devices in a mesh: dp: 32 (over z, y), tensor: 8 (over x, core).
Axes of the slice: x: 4, y: 4, z: 8, core: 2. Of those that a mesh axis runs over, the one named last changes fastest.
Arguments:
- out_grad: bfloat16 [8192, 4096], P('dp'), may hold values from -0.29882812 to 0.29882812
- hidden: bfloat16 [8192, 28672], P('dp', 'tensor'), may hold values from -60 to 60
- momentum: float32 [4096, 28672], P('dp', 'tensor'), may hold values from -48 to 48
- second: float32 [4096], P('dp'), may hold values from 0.01 to 0.2
Outputs:
- update: bfloat16 [4096, 28672], P('dp', 'tensor')
- momentum_out: float32 [4096, 28672], P('dp', 'tensor')
- second_out: float32 [4096], P('dp')
The draws below stay inside these ranges and needn't reach their ends.
All inputs are finite; a program needn't handle non-finite values.
Results may differ from the reference program's by a relative error of at most 0.035.
Values may be sent and summed in bfloat16 or wider, within the bound.
No kernel may reach another device: no remote copies, remote signals or barrier semaphores. Data moves between devices by JAX's collectives and lax.ppermute only.
A program may use at most 128 MiB of HBM per device.

```python
import math
import jax
import jax.numpy as jnp
from jax import lax

FF = 28672
ROWS_DEV = 128
ITERS = 3
ROWS = 4096
TOKENS = 8192
N_DP = 32


def draw_hidden(key, part):
    first_key = jax.random.fold_in(jax.random.fold_in(key, 17), 0)
    column_ramp = jnp.exp(jnp.log(3.0) * jnp.arange(FF, dtype=jnp.float32) / FF)
    base_values = jnp.clip(jax.random.normal(first_key, (TOKENS, FF), jnp.float32), -6.0, 6.0)
    return (base_values * column_ramp[None, :]).astype(jnp.bfloat16)


def with_spikes(drawn, stream_key, source, target, blocks, factor):
    owner, partner = [(jnp.arange(drawn.shape[position]) // (drawn.shape[position] // blocks)).reshape([-1 if axis == position else 1 for axis in range(drawn.ndim)]) for position in (source, target)]
    chosen = jax.random.permutation(stream_key, blocks)[partner]
    strong = (owner == chosen) | (owner == (partner + blocks // 2) % blocks)
    return jnp.where(strong, factor * drawn, drawn)


def shard_levels(own_key, dims, cuts, low, top_value):
    factor_of, own = 1.0, jax.random.fold_in(own_key, 6)
    for dim, shards_of in cuts:
        heights = jnp.exp(jax.random.uniform(jax.random.fold_in(own, dim), (shards_of,), jnp.float32, low / len(cuts), top_value / len(cuts)))
        factor_of = factor_of * jnp.repeat(heights, dims[dim] // shards_of).reshape([-1 if axis == dim else 1 for axis in range(len(dims))])
    return factor_of


def normal_values(rng, dims, width, limit, cuts=(), held_as=jnp.bfloat16):
    array = jax.random.normal(rng, dims, jnp.float32) * width
    if len(cuts) > 0:
        array = shard_levels(rng, dims, cuts, -0.22, 0.18) * array
    return jnp.clip(array, min=-limit, max=limit).astype(held_as)


def heavy_noise(stream_key, dims, width, bound, shards, heavy, kind=jnp.bfloat16):
    entries = width * jax.random.normal(stream_key, dims, jnp.float32)
    if shards:
        entries = entries * shard_levels(stream_key, dims, shards, -0.22, 0.18)
    return jnp.clip(with_spikes(entries, jax.random.fold_in(stream_key, 3), *heavy), -bound, bound).astype(kind)


def setup_inputs(seed: int = 0) -> dict:
    splits = jax.random.split(jax.random.key(seed), 5)
    out_grad = heavy_noise(splits[0], (TOKENS, ROWS), 0.05, 0.29882812, ((0, 32),), (0, 1, 32, 2.75))
    hidden = draw_hidden(jax.random.fold_in(splits[4], 71), 0)
    momentum = normal_values(splits[2], (ROWS, FF), 8.0, 48.0, ((0, 32), (1, 8)), jnp.float32)
    second = jnp.clip(jnp.exp(math.log(0.2) - 2.9957323 * jax.random.uniform(splits[3], (ROWS,), jnp.float32) ** shard_levels(splits[3], (ROWS,), ((0, 32),), -0.2, 0.2)), 0.01, 0.2)
    return dict(out_grad=out_grad, hidden=hidden, momentum=momentum, second=second)


quintic_a = 3.4445
quintic_b = -4.775
quintic_c = 2.0315
beta_one = 0.95
beta_two = 0.95

def orthogonal_panel(panel):
    norm_sum = jnp.sqrt(jnp.sum(panel * panel))
    current = (panel / (norm_sum + 1e-07)).astype(jnp.bfloat16)
    for iteration in range(ITERS):
        gram = jnp.dot(current, current.T, preferred_element_type=jnp.float32).astype(jnp.bfloat16)
        square = jnp.dot(gram, gram, preferred_element_type=jnp.float32)
        poly = (quintic_b * gram.astype(jnp.float32) + quintic_c * square).astype(jnp.bfloat16)
        current = (quintic_a * current.astype(jnp.float32) + jnp.dot(poly, current, preferred_element_type=jnp.float32)).astype(jnp.bfloat16)
    return current

def reference(out_grad, hidden, momentum, second):
    tok_block = out_grad.shape[0] // N_DP
    grad_blocks = out_grad.reshape(N_DP, tok_block, out_grad.shape[1])
    hidden_blocks = hidden.reshape(N_DP, tok_block, hidden.shape[1])

    def add_block(running, pair):
        grad_block, hidden_block = pair
        partial_term = lax.dot_general(grad_block, hidden_block, (((0,), (0,)), ((), ())), preferred_element_type=jnp.float32)
        rounded = lax.optimization_barrier(partial_term.astype(jnp.bfloat16))
        return (running + rounded.astype(jnp.float32), None)
    start_sum = jnp.zeros((out_grad.shape[1], hidden.shape[1]), jnp.float32)
    grad, unused = lax.scan(add_block, start_sum, (grad_blocks, hidden_blocks))
    momentum_out = beta_one * momentum + grad
    nesterov = grad + beta_one * momentum_out
    panels = nesterov.reshape(N_DP, ROWS_DEV, FF)
    orthogonal = lax.map(orthogonal_panel, panels).reshape(ROWS_DEV * N_DP, FF)
    ortho_wide = orthogonal.astype(jnp.float32)
    energy = lax.optimization_barrier(jnp.sum(ortho_wide * ortho_wide, axis=1))
    second_out = beta_two * second + (1.0 - beta_two) * energy
    update = (ortho_wide * jnp.sqrt(FF / second_out)[:, None]).astype(jnp.bfloat16)
    return (update, momentum_out, second_out)
```

```python
import jax
import jax.numpy as jnp
from jax import lax
from jax.experimental import pallas as pl
from jax.experimental.pallas import tpu as pltpu
from jax.sharding import Mesh, PartitionSpec as P

FF = 28672
ITERS = 3
quintic_a = 3.4445
quintic_b = -4.775
quintic_c = 2.0315
beta_one = 0.95
beta_two = 0.95
NZ, NY, NX, NC = 8, 4, 4, 2
SIZES = {"z": NZ, "y": NY, "x": NX, "core": NC}
TENSOR = ("x", "core")
CHUNKS = (512, 1024, 1024, 1024)
TILE = 512
PANEL = 128


def shifted(x, axis, by):
    count = SIZES[axis]
    return lax.ppermute(x, axis, [(i, (i + by) % count) for i in range(count)])


def exchanged_cotangent(out_grad):
    me_z, me_y, me_c = lax.axis_index("z"), lax.axis_index("y"), lax.axis_index("core")
    tokens = out_grad.shape[0]
    blocks = out_grad.reshape(tokens, NZ, NY, PANEL)
    twice = jnp.concatenate([blocks, blocks], axis=1)
    rolled = lax.dynamic_slice_in_dim(twice, me_z, NZ, axis=1)

    def rows_of(y):
        return lax.dynamic_index_in_dim(rolled, y, axis=2, keepdims=False).reshape(tokens, NZ * PANEL)

    own = rows_of(me_y)
    half = tokens // 2
    got = []
    for by in (1, -1, 2):
        block = rows_of((me_y + by) % NY)
        got.append(shifted(lax.dynamic_slice_in_dim(block, me_c * half, half, axis=0), "y", by))
    mine = jnp.stack(got)
    other = shifted(mine, "core", 1)
    first = jnp.where(me_c == 0, mine, other)
    second = jnp.where(me_c == 0, other, mine)
    rest = jnp.concatenate([first, second], axis=1).reshape(3 * tokens, NZ * PANEL)
    return jnp.concatenate([own, rest], axis=0)


def gathered_hidden(part):
    return jnp.concatenate([part] + [shifted(part, "y", by) for by in (1, -1, 2)], axis=0)


def scattered(c, long_plus):
    def block(i):
        return c[i * PANEL:(i + 1) * PANEL]

    def chain(order, by):
        v = block(order[0])
        for i in order[1:]:
            v = (shifted(v, "z", by).astype(jnp.float32) + block(i).astype(jnp.float32)).astype(jnp.bfloat16)
        return shifted(v, "z", by)

    if long_plus:
        up, down = chain((4, 3, 2, 1), 1), chain((5, 6, 7), -1)
    else:
        up, down = chain((3, 2, 1), 1), chain((4, 5, 6, 7), -1)
    return block(0), up, down


def blend_kernel(own, up, down, momentum, *rest):
    momentum_out, panel, gram = rest[-3:]
    grad = own[...].astype(jnp.float32) + up[...].astype(jnp.float32) + down[...].astype(jnp.float32)
    new = beta_one * momentum[...] + grad
    momentum_out[...] = new
    p = (grad + beta_one * new).astype(jnp.bfloat16)
    panel[...] = p
    g = lax.dot_general(p, p, (((1,), (1,)), ((), ())), preferred_element_type=jnp.float32)

    @pl.when(pl.program_id(0) == 0)
    def _():
        gram[...] = g if len(rest) == 3 else rest[1][...] + g

    @pl.when(pl.program_id(0) > 0)
    def _():
        gram[...] += g


def blended(own, up, down, momentum, start, previous):
    width = own.shape[1]
    local = pl.BlockSpec((PANEL, TILE), lambda j: (0, j))
    wide = pl.BlockSpec((PANEL, TILE), lambda j: (0, start // TILE + j))
    whole = pl.BlockSpec((PANEL, PANEL), lambda j: (0, 0))
    in_specs = [local, local, local, wide]
    args = [own, up, down, momentum]
    aliases = {}
    if previous is not None:
        in_specs += [pl.BlockSpec(memory_space=pl.ANY), whole]
        args += list(previous)
        aliases = {4: 0}
    return pl.pallas_call(
        blend_kernel,
        grid=(width // TILE,),
        in_specs=in_specs,
        out_specs=[wide, local, whole],
        out_shape=[
            jax.ShapeDtypeStruct(momentum.shape, jnp.float32),
            jax.ShapeDtypeStruct(own.shape, jnp.bfloat16),
            jax.ShapeDtypeStruct((PANEL, PANEL), jnp.float32),
        ],
        input_output_aliases=aliases,
        cost_estimate=pl.CostEstimate(flops=2 * PANEL * PANEL * width, bytes_accessed=PANEL * width * 16, transcendentals=0),
        name="blend",
    )(*args)


def finish_kernel(grams, second, *refs):
    panels, (update, second_out) = refs[:len(CHUNKS)], refs[len(CHUNKS):]
    hi = lax.Precision.HIGHEST

    def mul(a, b):
        return jnp.dot(a, b, precision=hi, preferred_element_type=jnp.float32)

    raw = jnp.sum(grams[...].astype(jnp.float32), axis=0)
    eye = lax.broadcasted_iota(jnp.int32, (PANEL, PANEL), 0) == lax.broadcasted_iota(jnp.int32, (PANEL, PANEL), 1)
    norm = jnp.sqrt(jnp.sum(jnp.where(eye, raw, 0.0), keepdims=True))
    scale = 1.0 / (norm + 1e-07)
    gram = raw * scale * scale
    unit = jnp.where(eye, quintic_a, 0.0)
    total = None
    for _ in range(ITERS):
        factor = unit + quintic_b * gram + quintic_c * mul(gram, gram)
        total = factor if total is None else mul(factor, total)
        gram = mul(mul(factor, gram), factor)
    energy = jnp.sum(jnp.where(eye, gram, 0.0), axis=1, keepdims=True)
    new = beta_two * second[...] + (1.0 - beta_two) * energy
    second_out[...] = new
    row = jnp.sqrt(FF / new)
    total = total * scale
    high = total.astype(jnp.bfloat16)
    low = (total - high.astype(jnp.float32)).astype(jnp.bfloat16)
    start = 0
    for panel in panels:
        p = panel[...]
        x = jnp.dot(high, p, preferred_element_type=jnp.float32) + jnp.dot(low, p, preferred_element_type=jnp.float32)
        x = x.astype(jnp.bfloat16).astype(jnp.float32)
        update[:, start:start + p.shape[1]] = (x * row).astype(jnp.bfloat16)
        start += p.shape[1]


def finished(grams, second, panels):
    columns = sum(p.shape[1] for p in panels)
    vmem = pl.BlockSpec(memory_space=pltpu.VMEM)
    update, second_out = pl.pallas_call(
        finish_kernel,
        in_specs=[vmem] * (2 + len(panels)),
        out_specs=[vmem, vmem],
        out_shape=[
            jax.ShapeDtypeStruct((PANEL, columns), jnp.bfloat16),
            jax.ShapeDtypeStruct((PANEL, 1), jnp.float32),
        ],
        compiler_params=pltpu.CompilerParams(vmem_limit_bytes=32 << 20),
        name="finish",
    )(grams, second[:, None], *panels)
    return update, second_out[:, 0]


def body(out_grad, hidden, momentum, second):
    a = exchanged_cotangent(out_grad)
    state, panels, start = None, [], 0
    for n, width in enumerate(CHUNKS):
        b = gathered_hidden(hidden[:, start:start + width])
        c = lax.dot_general(a, b, (((0,), (0,)), ((), ())), preferred_element_type=jnp.float32).astype(jnp.bfloat16)
        own, up, down = scattered(c, n % 2 == 0)
        momentum_out, panel, gram = blended(own, up, down, momentum, start, state)
        state = (momentum_out, gram)
        panels.append(panel)
        start += width
    momentum_out, gram = state
    grams = lax.all_to_all(jnp.broadcast_to(gram[None], (NX * NC, PANEL, PANEL)), TENSOR, 0, 0, tiled=True)
    update, second_out = finished(grams, second, panels)
    return update, momentum_out, second_out


def solution(mesh):
    cube = Mesh(mesh.devices.reshape(NZ, NY, NX, NC), ("z", "y", "x", "core"))
    dp = ("z", "y")
    placed = (P(dp, None), P(dp, TENSOR), P(dp, TENSOR), P(dp))
    return jax.shard_map(
        body,
        mesh=cube,
        in_specs=placed,
        out_specs=(P(dp, TENSOR), P(dp, TENSOR), P(dp)),
        check_vma=False,
    )
```

```python
import jax
import jax.numpy as jnp
from jax import lax
from jax.experimental import pallas as pl
from jax.experimental.pallas import tpu as pltpu
from jax.sharding import Mesh, PartitionSpec as P

FF = 28672
ITERS = 3
quintic_a = 3.4445
quintic_b = -4.775
quintic_c = 2.0315
beta_one = 0.95
beta_two = 0.95
NZ, NY, NX, NC = 8, 4, 4, 2
SIZES = {"z": NZ, "y": NY, "x": NX, "core": NC}
TENSOR = ("x", "core")
CHUNKS = (1024, 1280, 1280)
TILE = 256
ORDER = (
    "v0 n0 n1 w0", "f0 n2 f1 x0", "T0 o0 P0 a0", "b0 o1 P1 f2", "a1 c0 b1 d0", "c1 o2 P2 a2",
    "d1 b2 c2 d2",
)
DEPTH = 4
AHEAD = {"f2": 0}
INSTEAD = {}
PANEL = 128
TOKENS = 256
SHARE = TOKENS // (NX * NC)
DISTANCES = (3, 2, 1, 0, 4)
VMEM = pl.BlockSpec(memory_space=pltpu.VMEM)
SMEM = pl.BlockSpec(memory_space=pltpu.SMEM)
LIMIT = pltpu.CompilerParams(vmem_limit_bytes=40 << 20)


def shifted(x, axis, by):
    count = SIZES[axis]
    return lax.ppermute(x, axis, [(i, (i + by) % count) for i in range(count)])


def core_swapped(x):
    return lax.ppermute(x, "core", [(0, 1), (1, 0)])


def around(x, axis):
    count = SIZES[axis]
    pairs = [(2 * i + c, 2 * ((i + 1 - 2 * c) % count) + c) for i in range(count) for c in range(2)]
    return lax.ppermute(x, (axis, "core"), pairs)


def after(x, *others):
    return lax.optimization_barrier((x,) + others)[0]


def shape(*dims, dtype=jnp.bfloat16):
    return jax.ShapeDtypeStruct(dims, dtype)


def source_kernel(place, out_grad, above, below, across):
    y = place[1]
    for by, out in ((1, above), (NY - 1, below), (2, across)):
        target = lax.rem(y + by, NY)
        for z in range(NZ):
            lane = pl.multiple_of((z * NY + target) * PANEL, PANEL)
            out[:, z * PANEL:(z + 1) * PANEL] = out_grad[:, pl.ds(lane, PANEL)]


def source(place, out_grad):
    whole = pl.BlockSpec((SHARE, NZ * PANEL), lambda i, place: (0, 0))
    return pl.pallas_call(
        source_kernel,
        grid_spec=pltpu.PrefetchScalarGridSpec(
            num_scalar_prefetch=1,
            grid=(1,),
            in_specs=[pl.BlockSpec((SHARE, NZ * NY * PANEL), lambda i, place: (place[4], 0))],
            out_specs=[whole] * 3,
        ),
        out_shape=[shape(SHARE, NZ * PANEL)] * 3,
        name="source",
    )(place, out_grad)


def turn_kernel(place, out_grad, both, near, far, other, turned, spread):
    z, y, c, x = place[0], place[1], place[2], place[3]
    step = 1 - 2 * c
    shares = (
        (0, c, lambda k: both[0, k]), (0, 1 - c, lambda k: both[1, k]),
        (NX - step, c, lambda k: near[0, k]), (NX - step, 1 - c, lambda k: near[1, k]),
        (NX + step, c, lambda k: other[1, k]), (NX + step, 1 - c, lambda k: other[0, k]),
        (2, c, lambda k: far[k]), (2, 1 - c, lambda k: other[2, k]),
    )
    for chip, core, piece in shares:
        at = pl.multiple_of((lax.rem(x + chip, NX) * NC + core) * SHARE, SHARE)
        for k in range(NY - 1):
            spread[k, pl.ds(at, SHARE)] = piece(k)
    for i, distance in enumerate(DISTANCES):
        owner = lax.rem(z + step * distance + NZ, NZ)
        lane = pl.multiple_of((owner * NY + y) * PANEL, PANEL)
        rows = slice(i * PANEL, (i + 1) * PANEL)
        turned[rows, 0:TOKENS] = out_grad[:, pl.ds(lane, PANEL)].T
        lane = pl.multiple_of(owner * PANEL, PANEL)
        for k, of in enumerate((c, 1 - c, 2)):
            turned[rows, (k + 1) * TOKENS:(k + 2) * TOKENS] = spread[of, :, pl.ds(lane, PANEL)].T


def turned_cotangent(place, out_grad, *others):
    return pl.pallas_call(
        turn_kernel,
        in_specs=[SMEM] + [VMEM] * 5,
        out_specs=VMEM,
        out_shape=shape(len(DISTANCES) * PANEL, NY * TOKENS),
        scratch_shapes=[pltpu.VMEM((NY - 1, TOKENS, NZ * PANEL), jnp.bfloat16)],
        compiler_params=LIMIT,
        cost_estimate=pl.CostEstimate(flops=0, bytes_accessed=6 << 20, transcendentals=0),
        name="turn",
    )(place, out_grad, *others)


def product_kernel(turned, part, sibling, near, far, other, three, two, one, own, four):
    width = part.shape[1]

    def summed(rows, blocks):
        return jnp.dot(
            turned[0:rows], jnp.concatenate(blocks, axis=0), preferred_element_type=jnp.float32
        ).astype(jnp.bfloat16)

    @pl.loop(0, width // TILE)
    def _(j):
        at = pl.ds(pl.multiple_of(j * TILE, TILE), TILE)
        mine = summed(5 * PANEL, [part[:, at], near[0, :, at], other[1, :, at], far[:, at]])
        for i, out in enumerate((three, two, one)):
            out[0, :, at] = mine[i * PANEL:(i + 1) * PANEL]
        own[:, at] = mine[3 * PANEL:4 * PANEL]
        four[:, at] = mine[4 * PANEL:]
        theirs = summed(3 * PANEL, [sibling[:, at], near[1, :, at], other[0, :, at], other[2, :, at]])
        for i, out in enumerate((three, two, one)):
            out[1, :, at] = theirs[i * PANEL:(i + 1) * PANEL]


def product(turned, parts):
    width = parts[0].shape[1]
    flops = 2 * NY * TOKENS * NZ * PANEL * width
    return pl.pallas_call(
        product_kernel,
        in_specs=[VMEM] * 6,
        out_specs=[VMEM] * 5,
        out_shape=[shape(2, PANEL, width)] * 3 + [shape(PANEL, width)] * 2,
        compiler_params=LIMIT,
        cost_estimate=pl.CostEstimate(flops=flops, bytes_accessed=6 * TOKENS * width * 2, transcendentals=0),
        name="product",
    )(turned, *parts)


def added(x, y):
    return (x.astype(jnp.float32) + y.astype(jnp.float32)).astype(jnp.bfloat16)


def blend_kernel(*refs):
    n = len(CHUNKS)
    pieces, momentum, (momentum_out, panel, grams) = refs[:3 * n], refs[3 * n], refs[3 * n + 1:]
    gram, start = None, 0
    for i, width in enumerate(CHUNKS):
        own, ring, swapped = pieces[3 * i:3 * i + 3]
        at = slice(start, start + width)
        grad = own[...].astype(jnp.float32) + ring[0].astype(jnp.float32) + swapped[...].astype(jnp.float32)
        new = beta_one * momentum[:, at] + grad
        momentum_out[:, at] = new
        p = (grad + beta_one * new).astype(jnp.bfloat16)
        panel[:, at] = p
        g = lax.dot_general(p, p, (((1,), (1,)), ((), ())), preferred_element_type=jnp.float32)
        gram = g if gram is None else gram + g
        start += width
    gram = gram.astype(jnp.bfloat16)
    for i in range(NX * NC):
        grams[i] = gram


def blended(pieces, momentum):
    rows, columns = momentum.shape
    return pl.pallas_call(
        blend_kernel,
        in_specs=[VMEM] * (len(pieces) + 1),
        out_specs=[VMEM] * 3,
        out_shape=[shape(rows, columns, dtype=jnp.float32), shape(rows, columns), shape(NX * NC, rows, rows)],
        compiler_params=LIMIT,
        name="blend",
    )(*pieces, momentum)


def finish_kernel(grams, second, panel, update, second_out):
    def mul(a, b):
        return jnp.dot(a, b, precision=lax.Precision.HIGHEST, preferred_element_type=jnp.float32)

    raw = jnp.sum(grams[...].astype(jnp.float32), axis=0)
    eye = lax.broadcasted_iota(jnp.int32, (PANEL, PANEL), 0) == lax.broadcasted_iota(jnp.int32, (PANEL, PANEL), 1)
    norm = jnp.sqrt(jnp.sum(jnp.where(eye, raw, 0.0), keepdims=True))
    scale = 1.0 / (norm + 1e-07)
    gram = raw * scale * scale
    unit = jnp.where(eye, quintic_a, 0.0)
    total = None
    for _ in range(ITERS):
        factor = unit + quintic_b * gram + quintic_c * mul(gram, gram)
        total = factor if total is None else mul(factor, total)
        gram = mul(mul(factor, gram), factor)
    energy = jnp.sum(jnp.where(eye, gram, 0.0), axis=0, keepdims=True)
    new = beta_two * second[...] + (1.0 - beta_two) * energy
    second_out[...] = new
    row = jnp.sum(jnp.where(eye, jnp.sqrt(FF / new), 0.0), axis=1, keepdims=True)
    total = total * scale
    high = total.astype(jnp.bfloat16)
    low = (total - high.astype(jnp.float32)).astype(jnp.bfloat16)
    for start in range(0, panel.shape[1], 512):
        p = panel[:, start:start + 512]
        x = jnp.dot(high, p, preferred_element_type=jnp.float32) + jnp.dot(low, p, preferred_element_type=jnp.float32)
        x = x.astype(jnp.bfloat16).astype(jnp.float32)
        update[:, start:start + 512] = (x * row).astype(jnp.bfloat16)


def finished(grams, second, panel):
    update, second_out = pl.pallas_call(
        finish_kernel,
        in_specs=[VMEM] * 3,
        out_specs=[VMEM] * 2,
        out_shape=[shape(*panel.shape), shape(1, PANEL, dtype=jnp.float32)],
        compiler_params=LIMIT,
        name="finish",
    )(grams, second[None], panel)
    return update, second_out[0]


def body(out_grad, hidden, momentum, second):
    z, y, x, core = [lax.axis_index(name) for name in ("z", "y", "x", "core")]
    place = jnp.stack([z, y, core, x, x * NC + core]).astype(jnp.int32)
    n = len(CHUNKS)
    starts = [sum(CHUNKS[:i]) for i in range(n)]
    part = [hidden[:, i:i + width] for i, width in zip(starts, CHUNKS)]
    sibling, near, far, other, made, ring = [[None] * n for _ in range(6)]
    got = jnp.stack([shifted(a, "y", by) for a, by in zip(source(place, out_grad), (1, -1, 2))])
    both = jnp.stack([got, core_swapped(got)])
    for i in range(n):
        sibling[i] = core_swapped(after(part[i], sibling[i - 1]) if i else part[i])
    arrived = [got]

    named = {}

    def sent(send, x, *args):
        x = after(x, named[INSTEAD[act]] if act in INSTEAD else arrived[max(0, len(arrived) - DEPTH)])
        if act in AHEAD:
            x = after(x, made[AHEAD[act]][4])
        arrived.append(send(x, *args))
        named[act] = arrived[-1]
        return arrived[-1]

    def joined(near, far):
        return jnp.concatenate([near, far[None]], axis=0)

    for act in " ".join(ORDER).split():
        kind, i = act[0], int(act[1])
        if kind == "v":
            near_a = sent(around, both, "x")
        elif kind == "w":
            far_a = sent(around, near_a[0], "x")
        elif kind == "x":
            other_a = core_swapped(joined(near_a, far_a))
        elif kind == "T":
            turned = turned_cotangent(place, out_grad, both, near_a, far_a, other_a)
        elif kind == "n":
            near[i] = sent(around, jnp.stack([part[i], sibling[i]]), "y")
        elif kind == "f":
            far[i] = sent(around, near[i][0], "y")
        elif kind == "o":
            other[i] = core_swapped(joined(near[i], far[i]))
        elif kind == "P":
            made[i] = product(turned, (part[i], sibling[i], near[i], far[i], other[i]))
        elif kind == "a":
            ring[i] = sent(around, made[i][4], "z")
        elif kind == "b":
            three = made[i][0]
            ring[i] = sent(around, jnp.stack([added(ring[i], three[0]), three[1]]), "z")
        elif kind in "cd":
            ring[i] = sent(around, added(ring[i], made[i]["cd".index(kind) + 1]), "z")
    pieces = [x for i in range(n) for x in (made[i][3], ring[i], core_swapped(ring[i][1]))]
    momentum_out, panel, grams = blended(pieces, momentum)
    grams = lax.all_to_all(grams, TENSOR, 0, 0, tiled=True)
    update, second_out = finished(grams, second, panel)
    return update, momentum_out, second_out


def solution(mesh):
    cube = Mesh(mesh.devices.reshape(NZ, NY, NX, NC), ("z", "y", "x", "core"))
    dp = ("z", "y")
    placed = (P(dp, None), P(dp, TENSOR), P(dp, TENSOR), P(dp))
    return jax.shard_map(
        body,
        mesh=cube,
        in_specs=placed,
        out_specs=(P(dp, TENSOR), P(dp, TENSOR), P(dp)),
        check_vma=False,
    )
```

```python
import jax
import jax.numpy as jnp
from jax import lax
from jax.experimental import pallas as pl
from jax.experimental.pallas import tpu as pltpu
from jax.sharding import Mesh, PartitionSpec as P

FF = 28672
ITERS = 3
quintic_a = 3.4445
quintic_b = -4.775
quintic_c = 2.0315
beta_one = 0.95
beta_two = 0.95
NZ, NY, NX, NC = 8, 4, 4, 2
SIZES = {"z": NZ, "y": NY, "x": NX, "core": NC}
TENSOR = ("x", "core")
CHUNKS = (1024, 1280, 1280)
TILE = 256
ORDER = (
    "v0 n0 n1 w0", "f0 n2 f1 x0", "T0 o0 P0 a0", "b0 o1 P1 f2", "a1 c0 b1 d0", "c1 o2 P2 a2",
    "d1 b2 c2 d2",
)
DEPTH = 4
AHEAD = {"f2": 0}
INSTEAD = {}
PANEL = 128
TOKENS = 256
SHARE = TOKENS // (NX * NC)
DISTANCES = (3, 2, 1, 0, 4)
VMEM = pl.BlockSpec(memory_space=pltpu.VMEM)
SMEM = pl.BlockSpec(memory_space=pltpu.SMEM)
LIMIT = pltpu.CompilerParams(vmem_limit_bytes=40 << 20)


def shifted(x, axis, by):
    count = SIZES[axis]
    return lax.ppermute(x, axis, [(i, (i + by) % count) for i in range(count)])


def core_swapped(x):
    return lax.ppermute(x, "core", [(0, 1), (1, 0)])


def around(x, axis):
    count = SIZES[axis]
    pairs = [(2 * i + c, 2 * ((i + 1 - 2 * c) % count) + c) for i in range(count) for c in range(2)]
    return lax.ppermute(x, (axis, "core"), pairs)


def after(x, *others):
    return lax.optimization_barrier((x,) + others)[0]


def shape(*dims, dtype=jnp.bfloat16):
    return jax.ShapeDtypeStruct(dims, dtype)


def source_kernel(place, out_grad, above, below, across):
    y = place[1]
    for by, out in ((1, above), (NY - 1, below), (2, across)):
        target = lax.rem(y + by, NY)
        for z in range(NZ):
            lane = pl.multiple_of((z * NY + target) * PANEL, PANEL)
            out[:, z * PANEL:(z + 1) * PANEL] = out_grad[:, pl.ds(lane, PANEL)]


def source(place, out_grad):
    whole = pl.BlockSpec((SHARE, NZ * PANEL), lambda i, place: (0, 0))
    return pl.pallas_call(
        source_kernel,
        grid_spec=pltpu.PrefetchScalarGridSpec(
            num_scalar_prefetch=1,
            grid=(1,),
            in_specs=[pl.BlockSpec((SHARE, NZ * NY * PANEL), lambda i, place: (place[4], 0))],
            out_specs=[whole] * 3,
        ),
        out_shape=[shape(SHARE, NZ * PANEL)] * 3,
        name="source",
    )(place, out_grad)


def turn_kernel(place, out_grad, both, near, far, other, turned, spread):
    z, y, c, x = place[0], place[1], place[2], place[3]
    step = 1 - 2 * c
    shares = (
        (0, c, lambda k: both[0, k]), (0, 1 - c, lambda k: both[1, k]),
        (NX - step, c, lambda k: near[0, k]), (NX - step, 1 - c, lambda k: near[1, k]),
        (NX + step, c, lambda k: other[1, k]), (NX + step, 1 - c, lambda k: other[0, k]),
        (2, c, lambda k: far[k]), (2, 1 - c, lambda k: other[2, k]),
    )
    for chip, core, piece in shares:
        at = pl.multiple_of((lax.rem(x + chip, NX) * NC + core) * SHARE, SHARE)
        for k in range(NY - 1):
            spread[k, pl.ds(at, SHARE)] = piece(k)
    for i, distance in enumerate(DISTANCES):
        owner = lax.rem(z + step * distance + NZ, NZ)
        lane = pl.multiple_of((owner * NY + y) * PANEL, PANEL)
        rows = slice(i * PANEL, (i + 1) * PANEL)
        turned[rows, 0:TOKENS] = out_grad[:, pl.ds(lane, PANEL)].T
        lane = pl.multiple_of(owner * PANEL, PANEL)
        for k, of in enumerate((c, 1 - c, 2)):
            turned[rows, (k + 1) * TOKENS:(k + 2) * TOKENS] = spread[of, :, pl.ds(lane, PANEL)].T


def turned_cotangent(place, out_grad, *others):
    return pl.pallas_call(
        turn_kernel,
        in_specs=[SMEM] + [VMEM] * 5,
        out_specs=VMEM,
        out_shape=shape(len(DISTANCES) * PANEL, NY * TOKENS),
        scratch_shapes=[pltpu.VMEM((NY - 1, TOKENS, NZ * PANEL), jnp.bfloat16)],
        compiler_params=LIMIT,
        cost_estimate=pl.CostEstimate(flops=0, bytes_accessed=6 << 20, transcendentals=0),
        name="turn",
    )(place, out_grad, *others)


def product_kernel(turned, part, sibling, near, far, other, three, two, one, own, four):
    width = part.shape[1]

    def summed(rows, blocks):
        return jnp.dot(
            turned[0:rows], jnp.concatenate(blocks, axis=0), preferred_element_type=jnp.float32
        ).astype(jnp.bfloat16)

    @pl.loop(0, width // TILE)
    def _(j):
        at = pl.ds(pl.multiple_of(j * TILE, TILE), TILE)
        mine = summed(5 * PANEL, [part[:, at], near[0, :, at], other[1, :, at], far[:, at]])
        for i, out in enumerate((three, two, one)):
            out[0, :, at] = mine[i * PANEL:(i + 1) * PANEL]
        own[:, at] = mine[3 * PANEL:4 * PANEL]
        four[:, at] = mine[4 * PANEL:]
        theirs = summed(3 * PANEL, [sibling[:, at], near[1, :, at], other[0, :, at], other[2, :, at]])
        for i, out in enumerate((three, two, one)):
            out[1, :, at] = theirs[i * PANEL:(i + 1) * PANEL]


def product(turned, parts):
    width = parts[0].shape[1]
    flops = 2 * NY * TOKENS * NZ * PANEL * width
    return pl.pallas_call(
        product_kernel,
        in_specs=[VMEM] * 6,
        out_specs=[VMEM] * 5,
        out_shape=[shape(2, PANEL, width)] * 3 + [shape(PANEL, width)] * 2,
        compiler_params=LIMIT,
        cost_estimate=pl.CostEstimate(flops=flops, bytes_accessed=6 * TOKENS * width * 2, transcendentals=0),
        name="product",
    )(turned, *parts)


def added(x, y):
    return (x.astype(jnp.float32) + y.astype(jnp.float32)).astype(jnp.bfloat16)


def blend_kernel(*refs):
    n = len(CHUNKS)
    pieces, momentum, (momentum_out, panel, grams) = refs[:3 * n], refs[3 * n], refs[3 * n + 1:]
    gram, start = None, 0
    for i, width in enumerate(CHUNKS):
        own, ring, swapped = pieces[3 * i:3 * i + 3]
        at = slice(start, start + width)
        grad = own[...].astype(jnp.float32) + ring[0].astype(jnp.float32) + swapped[...].astype(jnp.float32)
        new = beta_one * momentum[:, at] + grad
        momentum_out[:, at] = new
        p = (grad + beta_one * new).astype(jnp.bfloat16)
        panel[:, at] = p
        g = lax.dot_general(p, p, (((1,), (1,)), ((), ())), preferred_element_type=jnp.float32)
        gram = g if gram is None else gram + g
        start += width
    gram = gram.astype(jnp.bfloat16)
    for i in range(NX * NC):
        grams[i] = gram


def blended(pieces, momentum):
    rows, columns = momentum.shape
    return pl.pallas_call(
        blend_kernel,
        in_specs=[VMEM] * (len(pieces) + 1),
        out_specs=[VMEM] * 3,
        out_shape=[shape(rows, columns, dtype=jnp.float32), shape(rows, columns), shape(NX * NC, rows, rows)],
        compiler_params=LIMIT,
        name="blend",
    )(*pieces, momentum)


def finish_kernel(grams, second, panel, update, second_out):
    def mul(a, b):
        return jnp.dot(a, b, precision=lax.Precision.HIGHEST, preferred_element_type=jnp.float32)

    raw = jnp.sum(grams[...].astype(jnp.float32), axis=0)
    eye = lax.broadcasted_iota(jnp.int32, (PANEL, PANEL), 0) == lax.broadcasted_iota(jnp.int32, (PANEL, PANEL), 1)
    norm = jnp.sqrt(jnp.sum(jnp.where(eye, raw, 0.0), keepdims=True))
    scale = 1.0 / (norm + 1e-07)
    gram = raw * scale * scale
    unit = jnp.where(eye, quintic_a, 0.0)
    total = None
    for _ in range(ITERS):
        factor = unit + quintic_b * gram + quintic_c * mul(gram, gram)
        total = factor if total is None else mul(factor, total)
        gram = mul(mul(factor, gram), factor)
    energy = jnp.sum(jnp.where(eye, gram, 0.0), axis=0, keepdims=True)
    new = beta_two * second[...] + (1.0 - beta_two) * energy
    second_out[...] = new
    row = jnp.sum(jnp.where(eye, jnp.sqrt(FF / new), 0.0), axis=1, keepdims=True)
    total = total * scale
    high = total.astype(jnp.bfloat16)
    low = (total - high.astype(jnp.float32)).astype(jnp.bfloat16)
    for start in range(0, panel.shape[1], 512):
        p = panel[:, start:start + 512]
        x = jnp.dot(high, p, preferred_element_type=jnp.float32) + jnp.dot(low, p, preferred_element_type=jnp.float32)
        x = x.astype(jnp.bfloat16).astype(jnp.float32)
        update[:, start:start + 512] = (x * row).astype(jnp.bfloat16)


def finished(grams, second, panel):
    update, second_out = pl.pallas_call(
        finish_kernel,
        in_specs=[VMEM] * 3,
        out_specs=[VMEM] * 2,
        out_shape=[shape(*panel.shape), shape(1, PANEL, dtype=jnp.float32)],
        compiler_params=LIMIT,
        name="finish",
    )(grams, second[None], panel)
    return update, second_out[0]


def body(out_grad, hidden, momentum, second):
    z, y, x, core = [lax.axis_index(name) for name in ("z", "y", "x", "core")]
    place = jnp.stack([z, y, core, x, x * NC + core]).astype(jnp.int32)
    n = len(CHUNKS)
    starts = [sum(CHUNKS[:i]) for i in range(n)]
    sources = source(place, out_grad)
    hidden = after(hidden, sources[0])
    part = [hidden[:, i:i + width] for i, width in zip(starts, CHUNKS)]
    sibling, near, far, other, made, ring = [[None] * n for _ in range(6)]
    got = jnp.stack([shifted(a, "y", by) for a, by in zip(sources, (1, -1, 2))])
    both = jnp.stack([got, core_swapped(got)])
    for i in range(n):
        sibling[i] = core_swapped(after(part[i], sibling[i - 1]) if i else part[i])
    arrived = [got]

    named = {}

    def sent(send, x, *args):
        x = after(x, named[INSTEAD[act]] if act in INSTEAD else arrived[max(0, len(arrived) - DEPTH)])
        if act in AHEAD:
            x = after(x, made[AHEAD[act]][4])
        arrived.append(send(x, *args))
        named[act] = arrived[-1]
        return arrived[-1]

    def joined(near, far):
        return jnp.concatenate([near, far[None]], axis=0)

    for act in " ".join(ORDER).split():
        kind, i = act[0], int(act[1])
        if kind == "v":
            near_a = sent(around, both, "x")
        elif kind == "w":
            far_a = sent(around, near_a[0], "x")
        elif kind == "x":
            other_a = core_swapped(joined(near_a, far_a))
        elif kind == "T":
            turned = turned_cotangent(place, out_grad, both, near_a, far_a, other_a)
        elif kind == "n":
            near[i] = sent(around, jnp.stack([part[i], sibling[i]]), "y")
        elif kind == "f":
            far[i] = sent(around, near[i][0], "y")
        elif kind == "o":
            other[i] = core_swapped(joined(near[i], far[i]))
        elif kind == "P":
            made[i] = product(turned, (part[i], sibling[i], near[i], far[i], other[i]))
        elif kind == "a":
            ring[i] = sent(around, made[i][4], "z")
        elif kind == "b":
            three = made[i][0]
            ring[i] = sent(around, jnp.stack([added(ring[i], three[0]), three[1]]), "z")
        elif kind in "cd":
            ring[i] = sent(around, added(ring[i], made[i]["cd".index(kind) + 1]), "z")
    pieces = [x for i in range(n) for x in (made[i][3], ring[i], core_swapped(ring[i][1]))]
    momentum_out, panel, grams = blended(pieces, momentum)
    grams = lax.all_to_all(grams, TENSOR, 0, 0, tiled=True)
    update, second_out = finished(grams, second, panel)
    return update, momentum_out, second_out


def solution(mesh):
    cube = Mesh(mesh.devices.reshape(NZ, NY, NX, NC), ("z", "y", "x", "core"))
    dp = ("z", "y")
    placed = (P(dp, None), P(dp, TENSOR), P(dp, TENSOR), P(dp))
    return jax.shard_map(
        body,
        mesh=cube,
        in_specs=placed,
        out_specs=(P(dp, TENSOR), P(dp, TENSOR), P(dp)),
        check_vma=False,
    )
```
